128 devices in a mesh: grp: 4 (over x_hi, core), reg: 32 (over z, x_lo, y).
Axes of the slice: x: 4 (x_hi: 2, x_lo: 2; x = x_hi * 2 + x_lo), y: 4, z: 4, core: 2. Of those that a mesh axis runs over, the one named last changes fastest.
Arguments:
- grain_pos: float32 [3, 2097152], P(None, ('grp', 'reg')), may hold values from -6 to 6
- grain_vel: float32 [3, 2097152], P(None, ('grp', 'reg')), may hold values from -6 to 6
- grain_vol: float32 [2097152], P(('grp', 'reg')), may hold values from 0.5 to 2
- drag_coef: float32 [2097152], P(('grp', 'reg')), may hold values from 0.2 to 2
- grain_count: int32 [128], P(('grp', 'reg')), may hold values from 0 to 16384, as said below
- contact_rows: int32 [8, 2097152], P(None, ('grp', 'reg')), may hold values from -1 to 255, as said below
- contact_stiff: float32 [8, 2097152], P(None, ('grp', 'reg')), may hold values from 0.05 to 0.5
- partner_block: int32 [16384], P(('grp', 'reg')), may hold values from 0 to 191, as said below
- halo_list: int32 [2, 524288], P(None, ('grp', 'reg')), may hold values from 0 to 16383, as said below
- grain_cell: int32 [2097152], P(('grp', 'reg')), may hold values from 0 to 127
- tile_cell_block: int32 [16384], P(('grp', 'reg')), may hold values from 0 to 2047
- pressure_old: float32 [128, 128, 512], P('reg'), may hold values from -6 to 6
- pressure_source: float32 [128, 128, 512], P('reg'), may hold values from -6 to 6
- solid_old: float32 [128, 128, 512], P('reg'), may hold values from 0 to 1.5
Outputs:
- new_vel: float32 [3, 2097152], P(None, ('grp', 'reg'))
The draws below stay inside these ranges and needn't reach their ends.
Inputs may be any that keep to these rules, and one draw needn't show every extreme that they name: `grain_count`: devices of the last grp index hold no grains; a device's live grains fill its first slots; some device holds 16384. `contact_rows`: for a live grain in block t, entries 0 to 127 name grains of block t and entries 128 to 255 name grains of block partner_block[t]; every named grain is live; -1 marks an empty slot. Entries of slots that are not live carry no meaning. `partner_block`: blocks below 128 are the device's own, the next 32 are those received from the lower region, the last 32 those from the upper region; a block holding live grains never names a region that does not exist. `halo_list`: every entry names a live grain of its device where the device holds grains, else 0.
All inputs are finite; a program needn't handle non-finite values.
Results may differ from the reference program's by a relative error of at most 0.0003.
Values sent between devices are 32-bit elements; how exact they have to be, the bound alone decides.
A program may use at most 64 MiB of HBM per device.

```python
import math
import jax
import jax.numpy as jnp
from jax import lax

CAP = 16384
BLOCK = 128
K = 8
ITERS = 4
CY = 128
CZ = 512
SLOTS = 2097152
TILES = 16384
HALO = 4096
HALOS = 524288
NX = 128
CELLS = 262144
N_GRP = 4
N_REG = 32
DEVICES = 128


def held_counts(key):
    count_key = jax.random.fold_in(key, 11)
    first_key, second_key = jax.random.split(count_key)
    device_ids = jnp.arange(DEVICES)
    drawn = jax.random.randint(first_key, (DEVICES,), CAP // 8, CAP + 1)
    fullest = jax.random.randint(second_key, (), 0, (N_GRP - 1) * N_REG)
    drawn = jnp.where(device_ids == fullest, CAP, drawn)
    return jnp.where(device_ids >= (N_GRP - 1) * N_REG, 0, drawn).astype(jnp.int32)


def partner_blocks(key):
    counts = held_counts(key)
    per_dev = CAP // BLOCK
    halo_blocks = HALO // BLOCK
    tile_ids = jnp.arange(TILES)
    device = tile_ids // per_dev
    tile_index = tile_ids % per_dev
    region = device % N_REG
    held_grains = counts[device]
    live_tiles = (held_grains + BLOCK - 1) // BLOCK
    subkeys = jax.random.split(jax.random.fold_in(key, 23), 4)
    own_pick = jax.random.randint(subkeys[0], (TILES,), 0, jnp.maximum(live_tiles, 1))
    lower_ok = region > 0
    upper_ok = region < N_REG - 1
    coin_flip = jax.random.randint(subkeys[1], (TILES,), 0, 2)
    go_upper = jnp.where(lower_ok & upper_ok, coin_flip == 1, upper_ok)
    side_pick = per_dev + jnp.where(go_upper, halo_blocks, 0) + jax.random.randint(subkeys[2], (TILES,), 0, halo_blocks)
    use_halo = jax.random.randint(subkeys[3], (TILES,), 0, 2) == 1
    chosen = jnp.where(use_halo, side_pick, own_pick)
    dead_tile = tile_index >= live_tiles
    filler = jnp.where(tile_index % 2 == 0, 0, per_dev + 2 * halo_blocks - 1)
    return jnp.where(dead_tile, filler, chosen).astype(jnp.int32)


def draw_grain_count(key, part):
    return held_counts(key)


def draw_partner_block(key, part):
    return partner_blocks(key)


def draw_contact_rows(key, part):
    counts = held_counts(key)
    blocks = partner_blocks(key)
    per_dev = CAP // BLOCK
    slot_ids = jnp.arange(SLOTS)
    device = slot_ids // CAP
    local_slot = slot_ids % CAP
    tile_index = local_slot // BLOCK
    held_grains = counts[device]
    partner = blocks[slot_ids // BLOCK]
    subkeys = jax.random.split(jax.random.fold_in(key, 37), 2)
    rows_drawn = jax.random.randint(subkeys[0], (K, SLOTS), 0, 2 * BLOCK)
    keep_slot = jax.random.randint(subkeys[1], (K, SLOTS), 0, 4) > 0
    target_block = jnp.where(rows_drawn < BLOCK, tile_index[None, :], partner[None, :])
    target_row = rows_drawn % BLOCK
    target_live = jnp.where(target_block < per_dev, target_block * BLOCK + target_row < held_grains[None, :], True)
    source_live = (local_slot < held_grains)[None, :]
    valid = keep_slot & target_live & source_live
    dead_fill = jnp.where(jnp.arange(K)[:, None] == 0, 2 * BLOCK - 1, -1)
    return jnp.where(source_live, jnp.where(valid, rows_drawn, -1), dead_fill).astype(jnp.int32)


def draw_halo_list(key, part):
    counts = held_counts(key)
    entry_ids = jnp.arange(HALOS)
    device = entry_ids // HALO
    held_grains = jnp.maximum(counts[device], 1)[None, :]
    drawn = jax.random.randint(jax.random.fold_in(key, 53), (2, HALOS), 0, held_grains)
    leading = (entry_ids % HALO == 0)[None, :] & (jnp.arange(2)[:, None] == 0)
    return jnp.where(leading, held_grains - 1, drawn).astype(jnp.int32)


def place_ends(values, key, least, largest):
    place = [jax.random.randint(jax.random.fold_in(key, axis), (), 0, length) for axis, length in enumerate(values.shape)]
    longest = values.shape.index(max(values.shape))
    beside = place[:longest] + [(place[longest] + 1) % values.shape[longest]] + place[longest + 1:]
    return values.at[tuple(place)].set(least).at[tuple(beside)].set(largest)


def steps_of(own_key, shape, cuts, low, top_value):
    def one(position, shards_of):
        steps = jax.random.uniform(jax.random.fold_in(jax.random.fold_in(own_key, 6), position), (shards_of,), jnp.float32, low / len(cuts), top_value / len(cuts))
        return jnp.repeat(jnp.exp(steps), shape[position] // shards_of).reshape((-1,) + (1,) * (len(shape) - position - 1))

    loudness = one(*cuts[0])
    for cut in cuts[1:]:
        loudness = loudness * one(*cut)
    return loudness


def scatter_about(key, dims, spread, reach, cuts=(), kind=jnp.bfloat16):
    array = spread * jax.random.normal(key, dims, jnp.float32)
    if cuts:
        array = array * steps_of(key, dims, cuts, -0.22, 0.18)
    return jnp.clip(array, -reach, reach).astype(kind)


def setup_inputs(seed: int = 0) -> dict:
    arg_keys = jax.random.split(jax.random.key(seed), 15)
    return {
        "grain_pos": scatter_about(arg_keys[0], (3, SLOTS), 1.0, 6.0, ((1, 128),), jnp.float32),
        "grain_vel": scatter_about(arg_keys[1], (3, SLOTS), 1.0, 6.0, ((1, 128),), jnp.float32),
        "grain_vol": jnp.clip(jnp.exp(math.log(2.0) - 1.3862944 * jax.random.uniform(arg_keys[2], (SLOTS,), jnp.float32) ** steps_of(arg_keys[2], (SLOTS,), ((0, 128),), -0.2, 0.2)), 0.5, 2.0),
        "drag_coef": jnp.clip(jnp.exp(math.log(2.0) - 2.3025851 * jax.random.uniform(arg_keys[3], (SLOTS,), jnp.float32) ** steps_of(arg_keys[3], (SLOTS,), ((0, 128),), -0.2, 0.2)), 0.2, 2.0),
        "grain_count": draw_grain_count(jax.random.fold_in(arg_keys[14], 71), 0),
        "contact_rows": draw_contact_rows(jax.random.fold_in(arg_keys[14], 71), 0),
        "contact_stiff": jnp.clip(jnp.exp(math.log(0.5) - 2.3025851 * jax.random.uniform(arg_keys[6], (K, SLOTS), jnp.float32) ** steps_of(arg_keys[6], (K, SLOTS), ((1, 128),), -0.2, 0.2)), 0.05, 0.5),
        "partner_block": draw_partner_block(jax.random.fold_in(arg_keys[14], 71), 0),
        "halo_list": draw_halo_list(jax.random.fold_in(arg_keys[14], 71), 0),
        "grain_cell": place_ends(jax.random.randint(arg_keys[9], (SLOTS,), 0, BLOCK), jax.random.fold_in(arg_keys[9], 1), 0, BLOCK - 1).astype(jnp.int32),
        "tile_cell_block": place_ends(jax.random.randint(arg_keys[10], (TILES,), 0, CELLS // BLOCK), jax.random.fold_in(arg_keys[10], 1), 0, (CELLS // BLOCK) - 1).astype(jnp.int32),
        "pressure_old": scatter_about(arg_keys[11], (NX, CY, CZ), 1.0, 6.0, ((0, 32),), jnp.float32),
        "pressure_source": scatter_about(arg_keys[12], (NX, CY, CZ), 1.0, 6.0, ((0, 32),), jnp.float32),
        "solid_old": jnp.clip(1.5 * jax.random.uniform(arg_keys[13], (NX, CY, CZ), jnp.float32) ** steps_of(arg_keys[13], (NX, CY, CZ), ((0, 32),), -0.2, 0.2), 0.0, 1.5),
    }


SPRING = 1.0
DAMPING = 0.5
TIME_STEP = 0.5


def neighbours(padded):
    summed = padded[2:, 1:-1, 1:-1] + padded[:-2, 1:-1, 1:-1]
    summed = summed + padded[1:-1, 2:, 1:-1] + padded[1:-1, :-2, 1:-1]
    return summed + padded[1:-1, 1:-1, 2:] + padded[1:-1, 1:-1, :-2]


def per_device(packed):
    extended, rows_dev, stiff_dev, blocks_dev = packed
    tiles_here = CAP // BLOCK
    grain_state = extended[:, :CAP]
    partner = jnp.take(extended.reshape(6, -1, BLOCK), blocks_dev, axis=1)
    paired = jnp.concatenate([grain_state.reshape(6, tiles_here, BLOCK), partner], 2)
    rows_tiled = rows_dev.reshape(K, tiles_here, BLOCK)
    stiff_tiled = stiff_dev.reshape(K, tiles_here, BLOCK)
    columns = jnp.arange(2 * BLOCK, dtype=jnp.int32)
    weights = jnp.zeros((tiles_here, BLOCK, 2 * BLOCK), jnp.float32)
    for slot_index in range(K):
        weights = weights + jnp.where(rows_tiled[slot_index][:, :, None] == columns, stiff_tiled[slot_index][:, :, None], jnp.float32(0.0))
    summed = jnp.einsum("tij,ctj->cti", weights, paired, precision=lax.Precision.HIGHEST)
    stiff_total = jnp.sum(jnp.where(rows_tiled >= 0, stiff_tiled, jnp.float32(0.0)), 0)
    own_rows = paired[:, :, :BLOCK]
    spring = SPRING * (stiff_total * own_rows[:3] - summed[:3])
    damper = DAMPING * (summed[3:] - stiff_total * own_rows[3:])
    return (spring + damper).reshape(3, CAP)


def reference(grain_pos, grain_vel, grain_vol, drag_coef, grain_count, contact_rows, contact_stiff, partner_block, halo_list, grain_cell, tile_cell_block, pressure_old, pressure_source, solid_old):
    live_mask = (jnp.arange(CAP, dtype=jnp.int32)[None, :] < grain_count[:, None]).astype(jnp.float32).reshape(SLOTS)
    grain_state = jnp.concatenate([grain_pos, grain_vel], 0).reshape(6, N_GRP, N_REG, CAP)
    halo_rows = halo_list.reshape(2, N_GRP, N_REG, HALO).astype(jnp.int32)
    downward = jnp.take_along_axis(grain_state, halo_rows[0][None], axis=3)
    upward = jnp.take_along_axis(grain_state, halo_rows[1][None], axis=3)
    from_lower = jnp.pad(upward, ((0, 0), (0, 0), (1, 0), (0, 0)))[:, :, :-1]
    from_upper = jnp.pad(downward, ((0, 0), (0, 0), (0, 1), (0, 0)))[:, :, 1:]
    extended = jnp.concatenate([grain_state, from_lower, from_upper], 3)
    extended = jnp.transpose(extended, (1, 2, 0, 3)).reshape(DEVICES, 6, CAP + 2 * HALO)
    rows_all = jnp.transpose(contact_rows.reshape(K, DEVICES, CAP), (1, 0, 2))
    stiff_all = jnp.transpose(contact_stiff.reshape(K, DEVICES, CAP), (1, 0, 2))
    blocks_all = partner_block.reshape(DEVICES, CAP // BLOCK)
    contact = lax.map(per_device, (extended, rows_all, stiff_all, blocks_all))
    contact = jnp.transpose(contact, (1, 0, 2)).reshape(3, SLOTS)
    slot_ids = jnp.arange(SLOTS, dtype=jnp.int32)
    device_ids = slot_ids // CAP
    block_of_slot = jnp.take(tile_cell_block, slot_ids // BLOCK).astype(jnp.int32)
    global_cell = ((device_ids % N_REG) * CELLS + block_of_slot * BLOCK + grain_cell).astype(jnp.int32)
    solid_now = jax.ops.segment_sum(grain_vol * live_mask, global_cell, num_segments=NX * CY * CZ).reshape(NX, CY, CZ)
    drag_sum = jax.ops.segment_sum(drag_coef * live_mask, global_cell, num_segments=NX * CY * CZ).reshape(NX, CY, CZ)
    porous = 1.0 / (1.0 + solid_now)
    diagonal = 6.0 * porous + drag_sum + 1.0
    driving = pressure_source + solid_now - solid_old
    pressure = pressure_old
    for sweep_index in range(ITERS):
        pressure = (driving + porous * neighbours(jnp.pad(pressure, 1))) / diagonal
    weight = 1.0 / (porous + drag_sum)
    padded = jnp.pad(pressure, 1)
    grad_x = 0.5 * (padded[2:, 1:-1, 1:-1] - padded[:-2, 1:-1, 1:-1])
    grad_y = 0.5 * (padded[1:-1, 2:, 1:-1] - padded[1:-1, :-2, 1:-1])
    grad_z = 0.5 * (padded[1:-1, 1:-1, 2:] - padded[1:-1, 1:-1, :-2])
    fields = jnp.stack([grad_x, grad_y, grad_z, weight]).reshape(4, -1)
    at_grain = jnp.take(fields, global_cell, axis=1)
    gradient = at_grain[:3]
    fluid_vel = -gradient * at_grain[3]
    force = contact - grain_vol * gradient + drag_coef * (fluid_vel - grain_vel)
    return (grain_vel + TIME_STEP * force / grain_vol) * live_mask
```

```python
import functools

import jax
import jax.numpy as jnp
from jax import lax
from jax.experimental import pallas as pl
from jax.experimental.pallas import tpu as pltpu
from jax.sharding import PartitionSpec as P

BLOCK = 128
ITERS = 4
SPRING = 1.0
DAMPING = 0.5
TIME_STEP = 0.5
GHOST = 8
PAD = 8
MESH = pl.DeviceIdType.MESH
F32 = jnp.float32
BF16 = jnp.bfloat16


def iota(shape, axis):
    return lax.broadcasted_iota(jnp.int32, shape, axis)


def split(values):
    high = values.astype(BF16)
    return high, (values - high.astype(F32)).astype(BF16)


def lanes_at(table, lane):
    return jnp.take_along_axis(table, lane, axis=1, mode="promise_in_bounds")


def kernel(
    count_s, partner_s, tile_s, tile_v, pos, vel, vol, drag, cell, rows, stiff, halo, p_old, source, solid_old,
    out,
    loads, ids_all, ids_sib, state, velocity, halo_row, halo_out, contact, pbuf, hbuf, src_v, old_v, coef_a, coef_b,
    fields, part_own, part_sent, part_got, send, recv, local,
):
    tiles, slot_count = vol.shape[0], rows.shape[0]
    planes, width_y, width_z = p_old.shape
    half = width_y // 2
    slab = half + GHOST
    per_row = width_z // BLOCK
    halo_blocks = halo.shape[1] // BLOCK
    group, region = lax.axis_index("grp"), lax.axis_index("reg")
    regions = lax.axis_size("reg")
    core = lax.rem(group, 2)
    sibling = {"grp": group + 1 - 2 * core}
    across = {"grp": lax.rem(group + 2, 4)}
    upper = {"reg": lax.rem(region + 1, regions)}
    lower = {"reg": lax.rem(region + regions - 1, regions)}
    first_y = pl.multiple_of(core * (half - GHOST), 8)
    count = count_s[0]

    def remote(index, src, dst, device):
        return pltpu.make_async_remote_copy(
            src_ref=src, dst_ref=dst, send_sem=send.at[index], recv_sem=recv.at[index],
            device_id=device, device_id_type=MESH,
        )

    barrier = pltpu.get_barrier_semaphore()
    for device in (sibling, across, upper, lower):
        pl.semaphore_signal(barrier, inc=1, device_id=device, device_id_type=MESH)

    inner = pl.ds(PAD, slab)
    rows_y = pl.ds(first_y, slab)
    load_p = pltpu.make_async_copy(p_old.at[:, rows_y, :], pbuf.at[0, :, inner, :], local.at[0])
    load_src = pltpu.make_async_copy(source.at[:, rows_y, :], src_v, local.at[1])
    load_old = pltpu.make_async_copy(solid_old.at[:, rows_y, :], old_v, local.at[2])
    load_p.start()
    load_src.start()
    load_old.start()

    cells = iota((BLOCK, BLOCK), 0)

    def deposit(step, carry):
        first = pl.multiple_of(step * 8, 8)
        cell8 = cell[pl.ds(first, 8), :]
        slot = first * BLOCK + iota((8, BLOCK), 0) * BLOCK + iota((8, BLOCK), 1)
        live = slot < count
        vol8 = jnp.where(live, vol[pl.ds(first, 8), :], 0.0)
        drag8 = jnp.where(live, drag[pl.ds(first, 8), :], 0.0)
        both = jnp.concatenate([vol8, drag8], 0)
        high, low = split(both)
        pieces = jnp.concatenate([high, low], 0)
        total = jnp.zeros((32, BLOCK), F32)
        for tile in range(8):
            hot = (cell8[tile : tile + 1, :] == cells).astype(F32).astype(BF16)
            found = lax.dot_general(pieces, hot, (((1,), (1,)), ((), ())), preferred_element_type=F32)
            total = jnp.where(iota((32, BLOCK), 0) % 8 == tile, found, total)
        total = total[:16] + total[16:]
        loads[0, pl.ds(first, 8), 0:BLOCK] = total[:8]
        loads[0, pl.ds(first, 8), BLOCK : 2 * BLOCK] = total[8:]
        return carry

    lax.fori_loop(0, tiles // 8, deposit, 0)
    ids_all[0] = tile_v[...]
    pl.semaphore_wait(barrier, 4)

    to_sibling = remote(0, loads.at[0], loads.at[1], sibling)
    to_across = remote(1, loads.at[0], loads.at[2], across)
    passed_on = remote(2, loads.at[2], loads.at[3], sibling)
    id_sibling = remote(3, tile_v, ids_all.at[1], sibling)
    id_across = remote(4, tile_v, ids_all.at[2], across)
    id_passed = remote(5, ids_all.at[2], ids_all.at[3], sibling)
    id_across.start()
    to_across.start()
    id_sibling.start()
    to_sibling.start()

    def planes_out(sweep):
        if sweep == 0:
            low, high = p_old.at[0, rows_y, :], p_old.at[planes - 1, rows_y, :]
        else:
            low, high = pbuf.at[sweep, 0, inner, :], pbuf.at[sweep, planes - 1, inner, :]
        return (
            remote(6 + 2 * sweep, low, hbuf.at[sweep, 1], lower),
            remote(7 + 2 * sweep, high, hbuf.at[sweep, 0], upper),
        )

    exchanges = [planes_out(sweep) for sweep in range(ITERS + 1)]
    for copy in exchanges[0]:
        copy.start()

    def tabulate(tile, carry):
        at = pl.ds(pl.multiple_of(tile * BLOCK, BLOCK), BLOCK)
        moved = vel[:, at]
        mixed = SPRING * pos[:, at] - DAMPING * moved
        for part in range(3):
            state[part, pl.ds(tile, 1), :] = mixed[part : part + 1]
            velocity[part, pl.ds(tile, 1), :] = moved[part : part + 1]
        return carry

    lax.fori_loop(0, tiles, tabulate, 0)

    def halo_rows(block, carry):
        at = pl.ds(pl.multiple_of(block * BLOCK, BLOCK), BLOCK)
        for side in range(2):
            halo_row[pl.ds(block + side * halo_blocks, 1), :] = halo[side : side + 1, at]
        return carry

    lax.fori_loop(0, halo_blocks, halo_rows, 0)
    wanted = halo_row[...]
    wanted_row, wanted_lane = wanted >> 7, wanted & (BLOCK - 1)

    def pick(row, picked):
        here = wanted_row == row
        return tuple(
            jnp.where(
                here,
                lanes_at(jnp.broadcast_to(state[part, pl.ds(row, 1), :], wanted.shape), wanted_lane),
                picked[part],
            )
            for part in range(3)
        )

    picked = lax.fori_loop(0, tiles, pick, tuple(jnp.zeros(wanted.shape, F32) for _ in range(3)))
    for part in range(3):
        for side in range(2):
            halo_out[side, part] = picked[part][side * halo_blocks : (side + 1) * halo_blocks]
    w_down = remote(16, halo_out.at[0], state.at[:, pl.ds(tiles + halo_blocks, halo_blocks), :], lower)
    w_up = remote(17, halo_out.at[1], state.at[:, pl.ds(tiles, halo_blocks), :], upper)
    w_down.start()
    w_up.start()

    id_across.wait_recv()
    id_passed.start()
    to_across.wait_recv()
    passed_on.start()

    for sweep in range(ITERS + 1):
        for plane in range(planes):
            pbuf[sweep, plane, 0:PAD, :] = jnp.zeros((PAD, width_z), F32)
            pbuf[sweep, plane, PAD + slab : 2 * PAD + slab, :] = jnp.zeros((PAD, width_z), F32)

    id_sibling.wait_recv()
    keep_ids = pltpu.make_async_copy(ids_all.at[1], ids_sib, local.at[3])
    keep_ids.start()
    id_passed.wait_recv()
    to_sibling.wait_recv()
    passed_on.wait_recv()
    load_p.wait()
    load_src.wait()
    load_old.wait()

    every = loads[...].reshape(4 * tiles, 2 * BLOCK)
    high, low = split(every)
    both = jnp.concatenate([high, low], 1)
    ids = jnp.concatenate([ids_all[source_id] for source_id in range(4)], 1)
    block_of = (iota((slab, 4 * tiles), 0) + first_y) * per_row
    for plane in range(planes):
        hot = jnp.concatenate(
            [
                (block_of + (plane * width_y * per_row + part) == ids).astype(F32).astype(BF16)
                for part in range(per_row)
            ],
            0,
        )
        placed = jnp.dot(hot, both, preferred_element_type=F32)
        placed = placed[:, : 2 * BLOCK] + placed[:, 2 * BLOCK :]
        for part in range(per_row):
            at = slice(part * BLOCK, (part + 1) * BLOCK)
            solid = placed[part * slab : (part + 1) * slab, :BLOCK]
            dragged = placed[part * slab : (part + 1) * slab, BLOCK:]
            porous = 1.0 / (1.0 + solid)
            inverse = 1.0 / (6.0 * porous + dragged + 1.0)
            driving = src_v[plane, :, at] + solid - old_v[plane, :, at]
            coef_a[plane, :, at] = driving * inverse
            coef_b[plane, :, at] = porous * inverse
            fields[(3 * planes + plane) * per_row + part] = 1.0 / (porous + dragged)

    lane = iota((slab, width_z), 1)

    def before_z(values):
        return jnp.where(lane == 0, 0.0, pltpu.roll(values, 1, 1))

    def after_z(values):
        return jnp.where(lane == width_z - 1, 0.0, pltpu.roll(values, width_z - 1, 1))

    def below(sweep, plane):
        if plane == 0:
            return jnp.where(region > 0, hbuf[sweep, 0], 0.0)
        return pbuf[sweep, plane - 1, PAD : PAD + slab, :]

    def above(sweep, plane):
        if plane == planes - 1:
            return jnp.where(region < regions - 1, hbuf[sweep, 1], 0.0)
        return pbuf[sweep, plane + 1, PAD : PAD + slab, :]

    def relax(sweep, plane):
        here = pbuf[sweep - 1, plane, PAD : PAD + slab, :]
        total = below(sweep - 1, plane) + above(sweep - 1, plane)
        total = total + pbuf[sweep - 1, plane, PAD - 1 : PAD + slab - 1, :]
        total = total + pbuf[sweep - 1, plane, PAD + 1 : PAD + slab + 1, :]
        total = total + before_z(here) + after_z(here)
        pbuf[sweep, plane, PAD : PAD + slab, :] = coef_a[plane] + coef_b[plane] * total

    def touch(tile, carry):
        at = pl.ds(pl.multiple_of(tile * BLOCK, BLOCK), BLOCK)
        row, strength = rows[:, at], stiff[:, at]
        strength = jnp.where(row >= 0, strength, 0.0)
        spot = row & (BLOCK - 1)
        own = row < BLOCK
        total = jnp.sum(strength, 0, keepdims=True)
        partner = partner_s[tile]
        for part in range(3):
            mine = state[part, pl.ds(tile, 1), :]
            theirs = state[part, pl.ds(partner, 1), :]
            found = jnp.where(
                own,
                lanes_at(jnp.broadcast_to(mine, row.shape), spot),
                lanes_at(jnp.broadcast_to(theirs, row.shape), spot),
            )
            contact[part, pl.ds(tile, 1), :] = total * mine - jnp.sum(strength * found, 0, keepdims=True)
        return carry

    w_down.wait_recv()
    w_up.wait_recv()
    share = tiles // ITERS
    for sweep in range(1, ITERS + 1):
        for plane in range(1, planes - 1):
            relax(sweep, plane)
        down, up = exchanges[sweep - 1]
        up.wait_recv()
        relax(sweep, 0)
        exchanges[sweep][0].start()
        down.wait_recv()
        relax(sweep, planes - 1)
        exchanges[sweep][1].start()
        lax.fori_loop((sweep - 1) * share, sweep * share, touch, 0)

    def keep(kind, plane, values):
        for part in range(per_row):
            fields[(kind * planes + plane) * per_row + part] = values[:, part * BLOCK : (part + 1) * BLOCK]

    def gradient(plane):
        here = pbuf[ITERS, plane, PAD : PAD + slab, :]
        after = pbuf[ITERS, plane, PAD + 1 : PAD + slab + 1, :]
        before = pbuf[ITERS, plane, PAD - 1 : PAD + slab - 1, :]
        keep(1, plane, 0.5 * (after - before))
        keep(2, plane, 0.5 * (after_z(here) - before_z(here)))

    for plane in range(planes):
        gradient(plane)
    keep_ids.wait()
    for copy in exchanges[ITERS]:
        copy.wait_recv()
    for plane in range(planes):
        keep(0, plane, 0.5 * (above(ITERS, plane) - below(ITERS, plane)))

    def take_block(block, part_ref, tile):
        plane, row, quarter = block // (width_y * per_row), (block // per_row) % width_y, block % per_row
        here = (row // half) == core
        row = jnp.clip(row - first_y, 0, slab - 1)
        for kind in range(4):
            found = fields[(kind * planes + plane) * per_row + quarter, pl.ds(row, 1), :]
            part_ref[kind, pl.ds(tile, 1), :] = jnp.where(here, found, 0.0)

    def take_tile(tile, carry):
        take_block(ids_sib[0, tile], part_sent, tile)
        return carry

    def take_own(tile, carry):
        take_block(tile_s[tile], part_own, tile)
        return carry

    lax.fori_loop(0, tiles, take_tile, 0)
    give = remote(18, part_sent, part_got, sibling)
    give.start()
    lax.fori_loop(0, tiles, take_own, 0)
    give.wait_recv()

    def finish(step, carry):
        first = pl.multiple_of(step * 8, 8)
        at = pl.ds(first, 8)
        slot = first * BLOCK + iota((8, BLOCK), 0) * BLOCK + iota((8, BLOCK), 1)
        live = slot < count
        where = cell[at, :]
        found = [lanes_at(part_own[kind, at, :] + part_got[kind, at, :], where) for kind in range(4)]
        vol8, drag8 = vol[at, :], drag[at, :]
        scale = TIME_STEP / vol8
        for part in range(3):
            slope, old = found[part], velocity[part, at, :]
            force = contact[part, at, :] - vol8 * slope + drag8 * (-slope * found[3] - old)
            out[part, at, :] = jnp.where(live, old + scale * force, 0.0)
        return carry

    lax.fori_loop(0, tiles // 8, finish, 0)

    sent = [to_sibling, to_across, passed_on, id_sibling, id_across, id_passed, w_down, w_up, give]
    for copy in sent + [copy for pair in exchanges for copy in pair]:
        copy.wait_send()


def on_device(
    grain_pos, grain_vel, grain_vol, drag_coef, grain_count, contact_rows, contact_stiff, partner_block, halo_list,
    grain_cell, tile_cell_block, pressure_old, pressure_source, solid_old,
):
    tiles = grain_vol.shape[0] // BLOCK
    planes, width_y, width_z = pressure_old.shape
    slab = width_y // 2 + GHOST
    halo_blocks = halo_list.shape[1] // BLOCK
    blocked = lambda flat: flat.reshape(tiles, BLOCK)
    vmem, smem, far = (pl.BlockSpec(memory_space=space) for space in (pltpu.VMEM, pltpu.SMEM, pl.ANY))
    copies = 9 + 2 * (ITERS + 1)
    out = pl.pallas_call(
        kernel,
        out_shape=jax.ShapeDtypeStruct((3, tiles, BLOCK), F32),
        in_specs=[smem] * 3 + [vmem] * 9 + [far] * 3,
        out_specs=vmem,
        scratch_shapes=[
            pltpu.VMEM((4, tiles, 2 * BLOCK), F32),
            pltpu.VMEM((4, 1, tiles), jnp.int32),
            pltpu.SMEM((1, tiles), jnp.int32),
            pltpu.VMEM((3, tiles + 2 * halo_blocks, BLOCK), F32),
            pltpu.VMEM((3, tiles, BLOCK), F32),
            pltpu.VMEM((2 * halo_blocks, BLOCK), jnp.int32),
            pltpu.VMEM((2, 3, halo_blocks, BLOCK), F32),
            pltpu.VMEM((3, tiles, BLOCK), F32),
            pltpu.VMEM((ITERS + 1, planes, slab + 2 * PAD, width_z), F32),
            pltpu.VMEM((ITERS + 1, 2, slab, width_z), F32),
            pltpu.VMEM((planes, slab, width_z), F32),
            pltpu.VMEM((planes, slab, width_z), F32),
            pltpu.VMEM((planes, slab, width_z), F32),
            pltpu.VMEM((planes, slab, width_z), F32),
            pltpu.VMEM((4 * planes * width_z // BLOCK, slab, BLOCK), F32),
            pltpu.VMEM((4, tiles, BLOCK), F32),
            pltpu.VMEM((4, tiles, BLOCK), F32),
            pltpu.VMEM((4, tiles, BLOCK), F32),
            pltpu.SemaphoreType.DMA((copies,)),
            pltpu.SemaphoreType.DMA((copies,)),
            pltpu.SemaphoreType.DMA((4,)),
        ],
        compiler_params=pltpu.CompilerParams(
            collective_id=0, has_side_effects=True, vmem_limit_bytes=56 * 1024 * 1024
        ),
        name="step",
    )(
        grain_count, partner_block, tile_cell_block, tile_cell_block.reshape(1, tiles), grain_pos, grain_vel,
        blocked(grain_vol), blocked(drag_coef), blocked(grain_cell), contact_rows, contact_stiff, halo_list,
        pressure_old, pressure_source, solid_old,
    )
    return out.reshape(3, tiles * BLOCK)


def solution(mesh):
    flat, wide = P(("grp", "reg")), P(None, ("grp", "reg"))
    field = P("reg", None, None)
    return jax.shard_map(
        on_device,
        mesh=mesh,
        in_specs=(wide, wide, flat, flat, flat, wide, wide, flat, wide, flat, flat, field, field, field),
        out_specs=wide,
        check_vma=False,
    )
```

```python
import functools

import jax
import jax.numpy as jnp
from jax import lax
from jax.experimental import pallas as pl
from jax.experimental.pallas import tpu as pltpu
from jax.sharding import PartitionSpec as P

BLOCK = 128
ITERS = 4
SPRING = 1.0
DAMPING = 0.5
TIME_STEP = 0.5
GHOST = 8
PAD = 8
MESH = pl.DeviceIdType.MESH
F32 = jnp.float32
BF16 = jnp.bfloat16


def iota(shape, axis):
    return lax.broadcasted_iota(jnp.int32, shape, axis)


def split(values):
    high = values.astype(BF16)
    return high, (values - high.astype(F32)).astype(BF16)


def lanes_at(table, lane):
    return jnp.take_along_axis(table, lane, axis=1, mode="promise_in_bounds")


def kernel(
    count_s, partner_s, tile_s, tile_v, pos, vel, vol, drag, cell, rows, stiff, halo, p_old, source, solid_old,
    out,
    loads, ids_all, ids_sib, state, velocity, halo_out, contact, pbuf, hbuf, src_v, old_v, coef_a, coef_b,
    fields, part_own, part_sent, part_got, send, recv, local,
):
    tiles, slot_count = vol.shape[0], rows.shape[0]
    planes, width_y, width_z = p_old.shape
    half = width_y // 2
    slab = half + GHOST
    per_row = width_z // BLOCK
    halo_blocks = halo.shape[1] // BLOCK
    group, region = lax.axis_index("grp"), lax.axis_index("reg")
    regions = lax.axis_size("reg")
    core = lax.rem(group, 2)
    sibling = {"grp": group + 1 - 2 * core}
    across = {"grp": lax.rem(group + 2, 4)}
    upper = {"reg": lax.rem(region + 1, regions)}
    lower = {"reg": lax.rem(region + regions - 1, regions)}
    first_y = pl.multiple_of(core * (half - GHOST), 8)
    count = count_s[0]

    def remote(index, src, dst, device):
        return pltpu.make_async_remote_copy(
            src_ref=src, dst_ref=dst, send_sem=send.at[index], recv_sem=recv.at[index],
            device_id=device, device_id_type=MESH,
        )

    barrier = pltpu.get_barrier_semaphore()
    for device in (sibling, across, upper, lower):
        pl.semaphore_signal(barrier, inc=1, device_id=device, device_id_type=MESH)

    inner = pl.ds(PAD, slab)
    rows_y = pl.ds(first_y, slab)
    load_p = pltpu.make_async_copy(p_old.at[:, rows_y, :], pbuf.at[0, :, inner, :], local.at[0])
    load_src = pltpu.make_async_copy(source.at[:, rows_y, :], src_v, local.at[1])
    load_old = pltpu.make_async_copy(solid_old.at[:, rows_y, :], old_v, local.at[2])
    load_p.start()
    load_src.start()
    load_old.start()

    cells = iota((BLOCK, BLOCK), 0)

    def deposit(step, carry):
        first = pl.multiple_of(step * 8, 8)
        cell8 = cell[pl.ds(first, 8), :]
        slot = first * BLOCK + iota((8, BLOCK), 0) * BLOCK + iota((8, BLOCK), 1)
        live = slot < count
        vol8 = jnp.where(live, vol[pl.ds(first, 8), :], 0.0)
        drag8 = jnp.where(live, drag[pl.ds(first, 8), :], 0.0)
        both = jnp.concatenate([vol8, drag8], 0)
        high, low = split(both)
        pieces = jnp.concatenate([high, low], 0)
        total = jnp.zeros((32, BLOCK), F32)
        for tile in range(8):
            hot = (cell8[tile : tile + 1, :] == cells).astype(F32).astype(BF16)
            found = lax.dot_general(pieces, hot, (((1,), (1,)), ((), ())), preferred_element_type=F32)
            total = jnp.where(iota((32, BLOCK), 0) % 8 == tile, found, total)
        total = total[:16] + total[16:]
        loads[0, pl.ds(first, 8), 0:BLOCK] = total[:8]
        loads[0, pl.ds(first, 8), BLOCK : 2 * BLOCK] = total[8:]
        return carry

    lax.fori_loop(0, tiles // 8, deposit, 0)
    ids_all[0] = tile_v[...]
    pl.semaphore_wait(barrier, 4)

    to_sibling = remote(0, loads.at[0], loads.at[1], sibling)
    to_across = remote(1, loads.at[0], loads.at[2], across)
    passed_on = remote(2, loads.at[2], loads.at[3], sibling)
    id_sibling = remote(3, tile_v, ids_all.at[1], sibling)
    id_across = remote(4, tile_v, ids_all.at[2], across)
    id_passed = remote(5, ids_all.at[2], ids_all.at[3], sibling)
    id_across.start()
    to_across.start()
    id_sibling.start()
    to_sibling.start()

    def planes_out(sweep):
        if sweep == 0:
            low, high = p_old.at[0, rows_y, :], p_old.at[planes - 1, rows_y, :]
        else:
            low, high = pbuf.at[sweep, 0, inner, :], pbuf.at[sweep, planes - 1, inner, :]
        return (
            remote(6 + 2 * sweep, low, hbuf.at[sweep, 1], lower),
            remote(7 + 2 * sweep, high, hbuf.at[sweep, 0], upper),
        )

    exchanges = [planes_out(sweep) for sweep in range(ITERS + 1)]
    for copy in exchanges[0]:
        copy.start()

    def tabulate(tile, carry):
        at = pl.ds(pl.multiple_of(tile * BLOCK, BLOCK), BLOCK)
        moved = vel[:, at]
        mixed = SPRING * pos[:, at] - DAMPING * moved
        for part in range(3):
            state[part, pl.ds(tile, 1), :] = mixed[part : part + 1]
            velocity[part, pl.ds(tile, 1), :] = moved[part : part + 1]
        return carry

    lax.fori_loop(0, tiles, tabulate, 0, unroll=4)

    pieces = []
    for part in range(3):
        high, low = split(state[part, 0:tiles, :].T)
        pieces.append(jnp.concatenate([high, low], 1))
    table = jnp.concatenate(pieces, 0)
    pair = 2 * BLOCK

    def pick(step, carry):
        at = pl.ds(pl.multiple_of(step * pair, pair), pair)
        for side in range(2):
            wanted = halo[side : side + 1, at]
            hot = ((iota((2 * tiles, pair), 0) & (tiles - 1)) == (wanted >> 7)).astype(F32).astype(BF16)
            found = jnp.dot(table, hot, preferred_element_type=F32)
            here = iota((BLOCK, pair), 0) == (wanted & (BLOCK - 1))
            for part in range(3):
                chosen = jnp.where(here, found[part * BLOCK : (part + 1) * BLOCK], 0.0)
                chosen = jnp.sum(chosen, 0, keepdims=True)
                halo_out[side, part, pl.ds(2 * step, 1), :] = chosen[:, :BLOCK]
                halo_out[side, part, pl.ds(2 * step + 1, 1), :] = chosen[:, BLOCK:]
        return carry

    lax.fori_loop(0, halo_blocks // 2, pick, 0)
    w_down = remote(16, halo_out.at[0], state.at[:, pl.ds(tiles + halo_blocks, halo_blocks), :], lower)
    w_up = remote(17, halo_out.at[1], state.at[:, pl.ds(tiles, halo_blocks), :], upper)
    w_down.start()
    w_up.start()

    id_across.wait_recv()
    id_passed.start()
    to_across.wait_recv()
    passed_on.start()

    for sweep in range(ITERS + 1):
        for plane in range(planes):
            pbuf[sweep, plane, 0:PAD, :] = jnp.zeros((PAD, width_z), F32)
            pbuf[sweep, plane, PAD + slab : 2 * PAD + slab, :] = jnp.zeros((PAD, width_z), F32)

    fields[:, slab : slab + PAD, :] = jnp.zeros((4 * planes * per_row, PAD, BLOCK), F32)
    id_sibling.wait_recv()
    keep_ids = pltpu.make_async_copy(ids_all.at[1], ids_sib, local.at[3])
    keep_ids.start()
    id_passed.wait_recv()
    to_sibling.wait_recv()
    passed_on.wait_recv()
    load_p.wait()
    load_src.wait()
    load_old.wait()

    every = loads[...].reshape(4 * tiles, 2 * BLOCK)
    high, low = split(every)
    both = jnp.concatenate([high, low], 1)
    ids = jnp.concatenate([ids_all[source_id] for source_id in range(4)], 1)
    block_of = (iota((slab, 4 * tiles), 0) + first_y) * per_row
    for plane in range(planes):
        hot = jnp.concatenate(
            [
                (block_of + (plane * width_y * per_row + part) == ids).astype(F32).astype(BF16)
                for part in range(per_row)
            ],
            0,
        )
        placed = jnp.dot(hot, both, preferred_element_type=F32)
        placed = placed[:, : 2 * BLOCK] + placed[:, 2 * BLOCK :]
        for part in range(per_row):
            at = slice(part * BLOCK, (part + 1) * BLOCK)
            solid = placed[part * slab : (part + 1) * slab, :BLOCK]
            dragged = placed[part * slab : (part + 1) * slab, BLOCK:]
            porous = 1.0 / (1.0 + solid)
            inverse = 1.0 / (6.0 * porous + dragged + 1.0)
            driving = src_v[plane, :, at] + solid - old_v[plane, :, at]
            coef_a[plane, :, at] = driving * inverse
            coef_b[plane, :, at] = porous * inverse
            fields[(3 * planes + plane) * per_row + part, 0:slab] = 1.0 / (porous + dragged)

    lane = iota((slab, width_z), 1)

    def before_z(values):
        return jnp.where(lane == 0, 0.0, pltpu.roll(values, 1, 1))

    def after_z(values):
        return jnp.where(lane == width_z - 1, 0.0, pltpu.roll(values, width_z - 1, 1))

    def below(sweep, plane):
        if plane == 0:
            return jnp.where(region > 0, hbuf[sweep, 0], 0.0)
        return pbuf[sweep, plane - 1, PAD : PAD + slab, :]

    def above(sweep, plane):
        if plane == planes - 1:
            return jnp.where(region < regions - 1, hbuf[sweep, 1], 0.0)
        return pbuf[sweep, plane + 1, PAD : PAD + slab, :]

    def relax(sweep, plane):
        here = pbuf[sweep - 1, plane, PAD : PAD + slab, :]
        total = below(sweep - 1, plane) + above(sweep - 1, plane)
        total = total + pbuf[sweep - 1, plane, PAD - 1 : PAD + slab - 1, :]
        total = total + pbuf[sweep - 1, plane, PAD + 1 : PAD + slab + 1, :]
        total = total + before_z(here) + after_z(here)
        pbuf[sweep, plane, PAD : PAD + slab, :] = coef_a[plane] + coef_b[plane] * total

    def touch(tile, carry):
        at = pl.ds(pl.multiple_of(tile * BLOCK, BLOCK), BLOCK)
        row, strength = rows[:, at], stiff[:, at]
        strength = jnp.where(row >= 0, strength, 0.0)
        spot = row & (BLOCK - 1)
        own = row < BLOCK
        total = jnp.sum(strength, 0, keepdims=True)
        partner = partner_s[tile]
        for part in range(3):
            mine = state[part, pl.ds(tile, 1), :]
            theirs = state[part, pl.ds(partner, 1), :]
            found = jnp.where(
                own,
                lanes_at(jnp.broadcast_to(mine, row.shape), spot),
                lanes_at(jnp.broadcast_to(theirs, row.shape), spot),
            )
            contact[part, pl.ds(tile, 1), :] = total * mine - jnp.sum(strength * found, 0, keepdims=True)
        return carry

    w_down.wait_recv()
    w_up.wait_recv()
    share = tiles // ITERS
    for sweep in range(1, ITERS + 1):
        for plane in range(1, planes - 1):
            relax(sweep, plane)
        down, up = exchanges[sweep - 1]
        up.wait_recv()
        relax(sweep, 0)
        exchanges[sweep][0].start()
        down.wait_recv()
        relax(sweep, planes - 1)
        exchanges[sweep][1].start()
        lax.fori_loop((sweep - 1) * share, sweep * share, touch, 0, unroll=4)

    def keep(kind, plane, values):
        for part in range(per_row):
            fields[(kind * planes + plane) * per_row + part, 0:slab] = values[:, part * BLOCK : (part + 1) * BLOCK]

    def gradient(plane):
        here = pbuf[ITERS, plane, PAD : PAD + slab, :]
        after = pbuf[ITERS, plane, PAD + 1 : PAD + slab + 1, :]
        before = pbuf[ITERS, plane, PAD - 1 : PAD + slab - 1, :]
        keep(1, plane, 0.5 * (after - before))
        keep(2, plane, 0.5 * (after_z(here) - before_z(here)))

    for plane in range(planes):
        gradient(plane)
    keep_ids.wait()
    for copy in exchanges[ITERS]:
        copy.wait_recv()
    for plane in range(planes):
        keep(0, plane, 0.5 * (above(ITERS, plane) - below(ITERS, plane)))

    bits_z, bits_y = per_row.bit_length() - 1, width_y.bit_length() - 1

    def take_block(block, part_ref, tile):
        quarter, row = block & (per_row - 1), (block >> bits_z) & (width_y - 1)
        plane = block >> (bits_z + bits_y)
        row = jnp.where((row >= half) == (core > 0), row - first_y, slab)
        for kind in range(4):
            part_ref[kind, pl.ds(tile, 1), :] = fields[kind * planes * per_row + plane * per_row + quarter, pl.ds(row, 1), :]

    def take_tile(tile, carry):
        take_block(ids_sib[0, tile], part_sent, tile)
        return carry

    def take_own(tile, carry):
        take_block(tile_s[tile], part_own, tile)
        return carry

    lax.fori_loop(0, tiles, take_tile, 0, unroll=8)
    give = remote(18, part_sent, part_got, sibling)
    give.start()
    lax.fori_loop(0, tiles, take_own, 0, unroll=8)
    give.wait_recv()

    def finish(step, carry):
        first = pl.multiple_of(step * 8, 8)
        at = pl.ds(first, 8)
        slot = first * BLOCK + iota((8, BLOCK), 0) * BLOCK + iota((8, BLOCK), 1)
        live = slot < count
        where = cell[at, :]
        found = [lanes_at(part_own[kind, at, :] + part_got[kind, at, :], where) for kind in range(4)]
        vol8, drag8 = vol[at, :], drag[at, :]
        scale = TIME_STEP / vol8
        for part in range(3):
            slope, old = found[part], velocity[part, at, :]
            force = contact[part, at, :] - vol8 * slope + drag8 * (-slope * found[3] - old)
            new = jnp.where(live, old + scale * force, 0.0)
            for tile in range(8):
                lanes = pl.ds(pl.multiple_of((first + tile) * BLOCK, BLOCK), BLOCK)
                out[part : part + 1, lanes] = new[tile : tile + 1]
        return carry

    lax.fori_loop(0, tiles // 8, finish, 0, unroll=2)

    sent = [to_sibling, to_across, passed_on, id_sibling, id_across, id_passed, w_down, w_up, give]
    for copy in sent + [copy for pair in exchanges for copy in pair]:
        copy.wait_send()


def on_device(
    grain_pos, grain_vel, grain_vol, drag_coef, grain_count, contact_rows, contact_stiff, partner_block, halo_list,
    grain_cell, tile_cell_block, pressure_old, pressure_source, solid_old,
):
    tiles = grain_vol.shape[0] // BLOCK
    planes, width_y, width_z = pressure_old.shape
    slab = width_y // 2 + GHOST
    halo_blocks = halo_list.shape[1] // BLOCK
    blocked = lambda flat: flat.reshape(tiles, BLOCK)
    vmem, smem, far = (pl.BlockSpec(memory_space=space) for space in (pltpu.VMEM, pltpu.SMEM, pl.ANY))
    copies = 9 + 2 * (ITERS + 1)
    out = pl.pallas_call(
        kernel,
        out_shape=jax.ShapeDtypeStruct((3, tiles * BLOCK), F32),
        in_specs=[smem] * 3 + [vmem] * 9 + [far] * 3,
        out_specs=vmem,
        scratch_shapes=[
            pltpu.VMEM((4, tiles, 2 * BLOCK), F32),
            pltpu.VMEM((4, 1, tiles), jnp.int32),
            pltpu.SMEM((1, tiles), jnp.int32),
            pltpu.VMEM((3, tiles + 2 * halo_blocks, BLOCK), F32),
            pltpu.VMEM((3, tiles, BLOCK), F32),
            pltpu.VMEM((2, 3, halo_blocks, BLOCK), F32),
            pltpu.VMEM((3, tiles, BLOCK), F32),
            pltpu.VMEM((ITERS + 1, planes, slab + 2 * PAD, width_z), F32),
            pltpu.VMEM((ITERS + 1, 2, slab, width_z), F32),
            pltpu.VMEM((planes, slab, width_z), F32),
            pltpu.VMEM((planes, slab, width_z), F32),
            pltpu.VMEM((planes, slab, width_z), F32),
            pltpu.VMEM((planes, slab, width_z), F32),
            pltpu.VMEM((4 * planes * width_z // BLOCK, slab + PAD, BLOCK), F32),
            pltpu.VMEM((4, tiles, BLOCK), F32),
            pltpu.VMEM((4, tiles, BLOCK), F32),
            pltpu.VMEM((4, tiles, BLOCK), F32),
            pltpu.SemaphoreType.DMA((copies,)),
            pltpu.SemaphoreType.DMA((copies,)),
            pltpu.SemaphoreType.DMA((4,)),
        ],
        compiler_params=pltpu.CompilerParams(
            collective_id=0, has_side_effects=True, vmem_limit_bytes=56 * 1024 * 1024
        ),
        name="step",
    )(
        grain_count, partner_block, tile_cell_block, tile_cell_block.reshape(1, tiles), grain_pos, grain_vel,
        blocked(grain_vol), blocked(drag_coef), blocked(grain_cell), contact_rows, contact_stiff, halo_list,
        pressure_old, pressure_source, solid_old,
    )
    return out


def solution(mesh):
    flat, wide = P(("grp", "reg")), P(None, ("grp", "reg"))
    field = P("reg", None, None)
    return jax.shard_map(
        on_device,
        mesh=mesh,
        in_specs=(wide, wide, flat, flat, flat, wide, wide, flat, wide, flat, flat, field, field, field),
        out_specs=wide,
        check_vma=False,
    )
```

```python
import functools

import jax
import jax.numpy as jnp
from jax import lax
from jax.experimental import pallas as pl
from jax.experimental.pallas import tpu as pltpu
from jax.sharding import PartitionSpec as P

BLOCK = 128
ITERS = 4
SPRING = 1.0
DAMPING = 0.5
TIME_STEP = 0.5
GHOST = 8
PAD = 8
MESH = pl.DeviceIdType.MESH
F32 = jnp.float32
BF16 = jnp.bfloat16


def iota(shape, axis):
    return lax.broadcasted_iota(jnp.int32, shape, axis)


def split(values):
    high = values.astype(BF16)
    return high, (values - high.astype(F32)).astype(BF16)


def lanes_at(table, lane):
    return jnp.take_along_axis(table, lane, axis=1, mode="promise_in_bounds")


def kernel(
    count_s, partner_s, tile_s, tile_v, vol, drag, cell, halo, pos_far, vel_far, rows_far, stiff_far, p_old, source, solid_old,
    out,
    pos, vel, rows, stiff, loads, ids_all, ids_sib, state, velocity, halo_out, contact, pbuf, near, deep, edge, src_v, old_v,
    coef, coef_got, fields, part_own, part_sent, part_got, send, recv, local,
):
    tiles, slot_count = vol.shape[0], rows.shape[0]
    planes, width_y, width_z = p_old.shape
    half = width_y // 2
    slab = half + GHOST
    per_row = width_z // BLOCK
    halo_blocks = halo.shape[1] // BLOCK
    group, region = lax.axis_index("grp"), lax.axis_index("reg")
    groups, regions = lax.axis_size("grp"), lax.axis_size("reg")
    core = lax.rem(group, 2)
    sibling_at, across_at = group + 1 - 2 * core, lax.rem(group + 2, groups)
    passed_at = lax.rem(sibling_at + 2, groups)
    sibling, across = {"grp": sibling_at}, {"grp": across_at}
    upper = {"reg": lax.rem(region + 1, regions)}
    lower = {"reg": lax.rem(region + regions - 1, regions)}
    has_lower, has_upper = region > 0, region < regions - 1
    last = groups - 1
    first_y = pl.multiple_of(core * (half - GHOST), 8)
    count = count_s[0]

    def remote(index, src, dst, device):
        return pltpu.make_async_remote_copy(
            src_ref=src, dst_ref=dst, send_sem=send.at[index], recv_sem=recv.at[index],
            device_id=device, device_id_type=MESH,
        )

    def greet(device):
        pl.semaphore_signal(barrier, inc=1, device_id=device, device_id_type=MESH)

    barrier = pltpu.get_barrier_semaphore()
    greet(sibling)
    greet(across)
    pl.when(has_lower)(lambda: greet(lower))
    pl.when(has_upper)(lambda: greet(upper))

    inner = pl.ds(PAD, slab)
    rows_y = pl.ds(first_y, slab)
    fetches = [
        pltpu.make_async_copy(src, dst, local.at[index])
        for index, (src, dst) in enumerate(
            [
                (pos_far, pos),
                (vel_far, vel),
                (p_old.at[:, rows_y, :], pbuf.at[0, :, inner, :]),
                (source.at[:, rows_y, :], src_v),
                (solid_old.at[:, rows_y, :], old_v),
                (rows_far, rows),
                (stiff_far, stiff),
            ]
        )
    ]
    for copy in fetches:
        copy.start()

    cells = iota((BLOCK, BLOCK), 0)

    def deposit(step, carry):
        first = pl.multiple_of(step * 8, 8)
        cell8 = cell[pl.ds(first, 8), :]
        slot = first * BLOCK + iota((8, BLOCK), 0) * BLOCK + iota((8, BLOCK), 1)
        live = slot < count
        vol8 = jnp.where(live, vol[pl.ds(first, 8), :], 0.0)
        drag8 = jnp.where(live, drag[pl.ds(first, 8), :], 0.0)
        both = jnp.concatenate([vol8, drag8], 0)
        high, low = split(both)
        pieces = jnp.concatenate([high, low], 0)
        total = jnp.zeros((32, BLOCK), F32)
        for tile in range(8):
            hot = (cell8[tile : tile + 1, :] == cells).astype(F32).astype(BF16)
            found = lax.dot_general(pieces, hot, (((1,), (1,)), ((), ())), preferred_element_type=F32)
            total = jnp.where(iota((32, BLOCK), 0) % 8 == tile, found, total)
        total = total[:16] + total[16:]
        loads[0, pl.ds(first, 8), 0:BLOCK] = total[:8]
        loads[0, pl.ds(first, 8), BLOCK : 2 * BLOCK] = total[8:]
        return carry

    lax.fori_loop(0, tiles // 8, deposit, 0)
    ids_all[0] = tile_v[...]
    pl.semaphore_wait(barrier, 2 + jnp.where(has_lower, 1, 0) + jnp.where(has_upper, 1, 0))

    to_sibling = remote(0, loads.at[0], loads.at[1], sibling)
    to_across = remote(1, loads.at[0], loads.at[2], across)
    passed_on = remote(2, loads.at[2], loads.at[3], sibling)
    id_sibling = remote(3, tile_v, ids_all.at[1], sibling)
    id_across = remote(4, tile_v, ids_all.at[2], across)
    id_passed = remote(5, ids_all.at[2], ids_all.at[3], sibling)

    def start(*copies):
        for copy in copies:
            copy.start()

    def arrive(*copies):
        for copy in copies:
            copy.wait_recv()

    def leave(*copies):
        for copy in copies:
            copy.wait_send()

    def blank(slot):
        loads[slot] = jnp.zeros((tiles, 2 * BLOCK), F32)
        ids_all[slot] = jnp.zeros((1, tiles), jnp.int32)

    sends = group != last
    pl.when(sends)(lambda: start(id_across, to_across, id_sibling, to_sibling))

    def planes_out(sweep):
        if sweep == 0:
            low, high = p_old.at[0, rows_y, :], p_old.at[planes - 1, rows_y, :]
        else:
            low, high = pbuf.at[sweep, 0, inner, :], pbuf.at[sweep, planes - 1, inner, :]
        return remote(6 + 2 * sweep, low, near.at[sweep, 1], lower), remote(7 + 2 * sweep, high, near.at[sweep, 0], upper)

    exchanges = [planes_out(sweep) for sweep in range(ITERS - 1)]
    deep_down = remote(12, pbuf.at[ITERS - 1, 0:2, inner, :], deep.at[1, :, inner, :], lower)
    deep_up = remote(13, pbuf.at[ITERS - 1, planes - 2 : planes, inner, :], deep.at[0, :, inner, :], upper)
    coef_down = remote(14, coef.at[0], coef_got.at[1], lower)
    coef_up = remote(15, coef.at[planes - 1], coef_got.at[0], upper)
    w_down = remote(16, halo_out.at[0], state.at[:, pl.ds(tiles + halo_blocks, halo_blocks), :], lower)
    w_up = remote(17, halo_out.at[1], state.at[:, pl.ds(tiles, halo_blocks), :], upper)
    pl.when(has_lower)(lambda: start(exchanges[0][0]))
    pl.when(has_upper)(lambda: start(exchanges[0][1]))
    fetches[0].wait()
    fetches[1].wait()

    def tabulate(tile, carry):
        at = pl.ds(pl.multiple_of(tile * BLOCK, BLOCK), BLOCK)
        moved = vel[:, at]
        mixed = SPRING * pos[:, at] - DAMPING * moved
        for part in range(3):
            state[part, pl.ds(tile, 1), :] = mixed[part : part + 1]
            velocity[part, pl.ds(tile, 1), :] = moved[part : part + 1]
        return carry

    lax.fori_loop(0, tiles, tabulate, 0, unroll=4)

    pieces = []
    for part in range(3):
        high, low = split(state[part, 0:tiles, :].T)
        pieces.append(jnp.concatenate([high, low], 1))
    table = jnp.concatenate(pieces, 0)
    pair = 2 * BLOCK

    def pick(step, carry):
        at = pl.ds(pl.multiple_of(step * pair, pair), pair)
        for side in range(2):
            wanted = halo[side : side + 1, at]
            hot = ((iota((2 * tiles, pair), 0) & (tiles - 1)) == (wanted >> 7)).astype(F32).astype(BF16)
            found = jnp.dot(table, hot, preferred_element_type=F32)
            here = iota((BLOCK, pair), 0) == (wanted & (BLOCK - 1))
            for part in range(3):
                chosen = jnp.where(here, found[part * BLOCK : (part + 1) * BLOCK], 0.0)
                chosen = jnp.sum(chosen, 0, keepdims=True)
                halo_out[side, part, pl.ds(2 * step, 1), :] = chosen[:, :BLOCK]
                halo_out[side, part, pl.ds(2 * step + 1, 1), :] = chosen[:, BLOCK:]
        return carry

    lax.fori_loop(0, halo_blocks // 2, pick, 0)
    pl.when(has_lower)(lambda: start(w_down))
    pl.when(has_upper)(lambda: start(w_up))

    @pl.when(across_at != last)
    def _():
        arrive(id_across, to_across)
        start(id_passed, passed_on)

    pl.when(across_at == last)(lambda: blank(2))
    pl.when(sibling_at == last)(lambda: blank(1))
    pl.when(passed_at == last)(lambda: blank(3))
    zero_rows = jnp.zeros((PAD, width_z), F32)
    for sweep in range(ITERS + 1):
        for plane in range(planes):
            pbuf[sweep, plane, 0:PAD, :] = zero_rows
            pbuf[sweep, plane, PAD + slab : 2 * PAD + slab, :] = zero_rows
    for side in range(2):
        for plane in range(2):
            deep[side, plane, 0:PAD, :] = zero_rows
            deep[side, plane, PAD + slab : 2 * PAD + slab, :] = zero_rows
    fields[:, slab : slab + PAD, :] = jnp.zeros((4 * planes * per_row, PAD, BLOCK), F32)

    def outside(side):
        for sweep in range(ITERS - 1):
            near[sweep, side] = jnp.zeros((slab, width_z), F32)
        for plane in range(2):
            deep[side, plane, PAD : PAD + slab, :] = jnp.zeros((slab, width_z), F32)
        edge[side] = jnp.zeros((slab, width_z), F32)
        at = pl.ds(tiles + side * halo_blocks, halo_blocks)
        state[:, at, :] = jnp.zeros((3, halo_blocks, BLOCK), F32)

    pl.when(jnp.logical_not(has_lower))(lambda: outside(0))
    pl.when(jnp.logical_not(has_upper))(lambda: outside(1))

    keep_ids = pltpu.make_async_copy(ids_all.at[1], ids_sib, local.at[7])

    @pl.when(sibling_at != last)
    def _():
        arrive(id_sibling)
        keep_ids.start()
        arrive(to_sibling)

    pl.when(passed_at != last)(lambda: arrive(id_passed, passed_on))
    for copy in fetches[2:5]:
        copy.wait()

    every = loads[...].reshape(4 * tiles, 2 * BLOCK)
    high, low = split(every)
    both = jnp.concatenate([high, low], 1)
    ids = jnp.concatenate([ids_all[source_id] for source_id in range(4)], 1)
    block_of = (iota((slab, 4 * tiles), 0) + first_y) * per_row

    def place(plane):
        hot = jnp.concatenate(
            [
                (block_of + (plane * width_y * per_row + part) == ids).astype(F32).astype(BF16)
                for part in range(per_row)
            ],
            0,
        )
        placed = jnp.dot(hot, both, preferred_element_type=F32)
        placed = placed[:, : 2 * BLOCK] + placed[:, 2 * BLOCK :]
        for part in range(per_row):
            at = slice(part * BLOCK, (part + 1) * BLOCK)
            solid = placed[part * slab : (part + 1) * slab, :BLOCK]
            dragged = placed[part * slab : (part + 1) * slab, BLOCK:]
            porous = 1.0 / (1.0 + solid)
            inverse = 1.0 / (6.0 * porous + dragged + 1.0)
            driving = src_v[plane, :, at] + solid - old_v[plane, :, at]
            coef[plane, 0, :, at] = driving * inverse
            coef[plane, 1, :, at] = porous * inverse
            fields[(3 * planes + plane) * per_row + part, 0:slab] = 1.0 / (porous + dragged)

    lane = iota((slab, width_z), 1)

    def before_z(values):
        return jnp.where(lane == 0, 0.0, pltpu.roll(values, 1, 1))

    def after_z(values):
        return jnp.where(lane == width_z - 1, 0.0, pltpu.roll(values, width_z - 1, 1))

    def middle(sweep, plane):
        if 0 <= plane < planes:
            return pbuf[sweep, plane, PAD : PAD + slab, :]
        if sweep < ITERS - 1:
            return near[sweep, 0 if plane < 0 else 1]
        if sweep == ITERS:
            return edge[0 if plane < 0 else 1]
        side, place_in = (0, plane + 2) if plane < 0 else (1, plane - planes)
        return deep[side, place_in, PAD : PAD + slab, :]

    def relax(sweep, plane):
        old = sweep - 1
        if 0 <= plane < planes:
            home, mine = pbuf.at[old, plane], coef.at[plane]
        else:
            home = deep.at[0, 1] if plane < 0 else deep.at[1, 0]
            mine = coef_got.at[0 if plane < 0 else 1]
        here = home[PAD : PAD + slab, :]
        total = middle(old, plane - 1) + middle(old, plane + 1)
        total = total + home[PAD - 1 : PAD + slab - 1, :] + home[PAD + 1 : PAD + slab + 1, :]
        total = total + before_z(here) + after_z(here)
        relaxed = mine[0] + mine[1] * total
        if 0 <= plane < planes:
            pbuf[sweep, plane, PAD : PAD + slab, :] = relaxed
        else:
            edge[0 if plane < 0 else 1] = relaxed

    def touch(tile, carry):
        at = pl.ds(pl.multiple_of(tile * BLOCK, BLOCK), BLOCK)
        row, strength = rows[:, at], stiff[:, at]
        strength = jnp.where(row >= 0, strength, 0.0)
        spot = row & (BLOCK - 1)
        own = row < BLOCK
        total = jnp.sum(strength, 0, keepdims=True)
        partner = partner_s[tile]
        for part in range(3):
            mine = state[part, pl.ds(tile, 1), :]
            theirs = state[part, pl.ds(partner, 1), :]
            found = jnp.where(
                own,
                lanes_at(jnp.broadcast_to(mine, row.shape), spot),
                lanes_at(jnp.broadcast_to(theirs, row.shape), spot),
            )
            contact[part, pl.ds(tile, 1), :] = total * mine - jnp.sum(strength * found, 0, keepdims=True)
        return carry

    def touches(step, carry):
        for tile in range(4):
            touch(4 * step + tile, carry)
        return carry

    top = planes - 1

    def ends(sweep):
        down, up = exchanges[sweep - 1]
        pl.when(has_lower)(lambda: arrive(up))
        relax(sweep, 0)
        if sweep < ITERS - 1:
            pl.when(has_lower)(lambda: start(exchanges[sweep][0]))
        pl.when(has_upper)(lambda: arrive(down))
        relax(sweep, top)
        if sweep < ITERS - 1:
            pl.when(has_upper)(lambda: start(exchanges[sweep][1]))

    def inside(sweep):
        for plane in range(1, top):
            relax(sweep, plane)

    share = tiles // (ITERS - 1)
    shares = [0, share // 2, tiles // 2, tiles]

    def contacts(step):
        lax.fori_loop(shares[step - 1] // 4, shares[step] // 4, touches, 0)

    place(0)
    place(top)
    ends(1)
    pl.when(has_lower)(lambda: start(coef_down))
    pl.when(has_upper)(lambda: start(coef_up))
    for plane in range(1, top):
        place(plane)
    inside(1)
    fetches[5].wait()
    fetches[6].wait()
    pl.when(has_lower)(lambda: arrive(w_up))
    pl.when(has_upper)(lambda: arrive(w_down))
    contacts(1)
    ends(2)
    inside(2)
    contacts(2)
    inside(3)
    ends(3)
    pl.when(has_lower)(lambda: start(deep_down))
    pl.when(has_upper)(lambda: start(deep_up))
    inside(4)
    contacts(3)

    def keep(kind, plane, values):
        for part in range(per_row):
            fields[(kind * planes + plane) * per_row + part, 0:slab] = values[:, part * BLOCK : (part + 1) * BLOCK]

    def gradient(plane):
        here = pbuf[ITERS, plane, PAD : PAD + slab, :]
        after = pbuf[ITERS, plane, PAD + 1 : PAD + slab + 1, :]
        before = pbuf[ITERS, plane, PAD - 1 : PAD + slab - 1, :]
        keep(1, plane, 0.5 * (after - before))
        keep(2, plane, 0.5 * (after_z(here) - before_z(here)))

    for plane in range(1, top):
        gradient(plane)

    @pl.when(has_lower)
    def _():
        arrive(deep_up, coef_up)
        relax(ITERS, -1)

    relax(ITERS, 0)

    @pl.when(has_upper)
    def _():
        arrive(deep_down, coef_down)
        relax(ITERS, planes)

    relax(ITERS, top)
    gradient(0)
    gradient(top)
    for plane in range(planes):
        keep(0, plane, 0.5 * (middle(ITERS, plane + 1) - middle(ITERS, plane - 1)))

    bits_z, bits_y = per_row.bit_length() - 1, width_y.bit_length() - 1

    def take_block(block, part_ref, tile):
        quarter, row = block & (per_row - 1), (block >> bits_z) & (width_y - 1)
        plane = block >> (bits_z + bits_y)
        row = jnp.where((row >= half) == (core > 0), row - first_y, slab)
        for kind in range(4):
            part_ref[kind, pl.ds(tile, 1), :] = fields[kind * planes * per_row + plane * per_row + quarter, pl.ds(row, 1), :]

    def take_tile(tile, carry):
        take_block(ids_sib[0, tile], part_sent, tile)
        return carry

    def take_own(tile, carry):
        take_block(tile_s[tile], part_own, tile)
        return carry

    give = remote(18, part_sent, part_got, sibling)

    @pl.when(sibling_at != last)
    def _():
        keep_ids.wait()
        lax.fori_loop(0, tiles, take_tile, 0, unroll=8)
        give.start()

    lax.fori_loop(0, tiles, take_own, 0, unroll=8)
    pl.when(sends)(lambda: arrive(give))

    def finish(step, carry):
        first = pl.multiple_of(step * 8, 8)
        at = pl.ds(first, 8)
        slot = first * BLOCK + iota((8, BLOCK), 0) * BLOCK + iota((8, BLOCK), 1)
        live = slot < count
        where = cell[at, :]
        found = [lanes_at(part_own[kind, at, :] + part_got[kind, at, :], where) for kind in range(4)]
        vol8, drag8 = vol[at, :], drag[at, :]
        scale = TIME_STEP / vol8
        for part in range(3):
            slope, old = found[part], velocity[part, at, :]
            force = contact[part, at, :] - vol8 * slope + drag8 * (-slope * found[3] - old)
            new = jnp.where(live, scale * force, -old)
            for tile in range(8):
                lanes = pl.ds(pl.multiple_of((first + tile) * BLOCK, BLOCK), BLOCK)
                out[part : part + 1, lanes] = new[tile : tile + 1]
        return carry

    lax.fori_loop(0, tiles // 8, finish, 0, unroll=2)

    pl.when(sends)(lambda: leave(id_across, to_across, id_sibling, to_sibling))
    pl.when(across_at != last)(lambda: leave(id_passed, passed_on))
    pl.when(sibling_at != last)(lambda: leave(give))
    pl.when(has_lower)(lambda: leave(*[down for down, up in exchanges], deep_down, coef_down, w_down))
    pl.when(has_upper)(lambda: leave(*[up for down, up in exchanges], deep_up, coef_up, w_up))


def on_device(
    grain_pos, grain_vel, grain_vol, drag_coef, grain_count, contact_rows, contact_stiff, partner_block, halo_list,
    grain_cell, tile_cell_block, pressure_old, pressure_source, solid_old,
):
    tiles = grain_vol.shape[0] // BLOCK
    planes, width_y, width_z = pressure_old.shape
    slab = width_y // 2 + GHOST
    halo_blocks = halo_list.shape[1] // BLOCK
    blocked = lambda flat: flat.reshape(tiles, BLOCK)
    vmem, smem, far = (pl.BlockSpec(memory_space=space) for space in (pltpu.VMEM, pltpu.SMEM, pl.ANY))
    copies = 19
    sheet = (slab, width_z)
    scratch = [
        ((3, tiles * BLOCK), F32),
        ((3, tiles * BLOCK), F32),
        (contact_rows.shape, jnp.int32),
        (contact_rows.shape, F32),
        ((4, tiles, 2 * BLOCK), F32),
        ((4, 1, tiles), jnp.int32),
        None,
        ((3, tiles + 2 * halo_blocks, BLOCK), F32),
        ((3, tiles, BLOCK), F32),
        ((2, 3, halo_blocks, BLOCK), F32),
        ((3, tiles, BLOCK), F32),
        ((ITERS + 1, planes, slab + 2 * PAD, width_z), F32),
        ((ITERS - 1, 2) + sheet, F32),
        ((2, 2, slab + 2 * PAD, width_z), F32),
        ((2,) + sheet, F32),
        ((planes,) + sheet, F32),
        ((planes,) + sheet, F32),
        ((planes, 2) + sheet, F32),
        ((2, 2) + sheet, F32),
        ((4 * planes * width_z // BLOCK, slab + PAD, BLOCK), F32),
        ((4, tiles, BLOCK), F32),
        ((4, tiles, BLOCK), F32),
        ((4, tiles, BLOCK), F32),
    ]
    change = pl.pallas_call(
        kernel,
        out_shape=jax.ShapeDtypeStruct((3, tiles * BLOCK), F32),
        in_specs=[smem] * 3 + [vmem] * 5 + [far] * 7,
        out_specs=vmem,
        scratch_shapes=[pltpu.SMEM((1, tiles), jnp.int32) if one is None else pltpu.VMEM(*one) for one in scratch]
        + [pltpu.SemaphoreType.DMA((copies,)), pltpu.SemaphoreType.DMA((copies,)), pltpu.SemaphoreType.DMA((8,))],
        compiler_params=pltpu.CompilerParams(
            collective_id=0, has_side_effects=True, vmem_limit_bytes=56 * 1024 * 1024
        ),
        name="step",
    )(
        grain_count, partner_block, tile_cell_block, tile_cell_block.reshape(1, tiles),
        blocked(grain_vol), blocked(drag_coef), blocked(grain_cell), halo_list, grain_pos, grain_vel,
        contact_rows, contact_stiff, pressure_old, pressure_source, solid_old,
    )
    return grain_vel + change


def solution(mesh):
    flat, wide = P(("grp", "reg")), P(None, ("grp", "reg"))
    field = P("reg", None, None)
    return jax.shard_map(
        on_device,
        mesh=mesh,
        in_specs=(wide, wide, flat, flat, flat, wide, wide, flat, wide, flat, flat, field, field, field),
        out_specs=wide,
        check_vma=False,
    )
```
